32 devices in a mesh: days: 2 (over x), chan: 4 (over y, core), sect: 4 (over z).
Axes of the slice: x: 2, y: 2, z: 4, core: 2. Of those that a mesh axis runs over, the one named last changes fastest.
Arguments:
- traces: bfloat16 [8, 256, 512], P(('days', 'sect'), 'chan'), parts along dimension 0, may hold values from -6 to 6
- positions: int32 [4, 256], replicated, may hold values from 0 to 255, each once within a row
- partners: int32 [4, 2], replicated, may hold values from 0 to 3, as said below
Outputs:
- stacks: float32 [8, 256, 3, 128], P(('days', 'sect'), 'chan'), parts along dimension 0
The draws below stay inside these ranges and needn't reach their ends.
There are 2 independent parts, one for each index of `days`. The reference program is written for one: setup_inputs(seed, part) draws one part's arguments, and reference() takes and returns one part's arrays. A program takes and returns all parts, laid end to end along the dimension named above; an argument that names none is the same for every part. Nothing has to cross between parts.
Inputs may be any that keep to these rules, and one draw needn't show every extreme that they name: Each row is a permutation of the positions 0 to 255. The sections stand in a circle in some order and r is one round from 1 to 3; partners[s] are the sections r places after and r places before s on that circle (the same section when r = 2), never s itself.
All inputs are finite; a program needn't handle non-finite values.
Results may differ from the reference program's by a relative error of at most 0.0003.
Values may be sent and summed in bfloat16 or wider, within the bound.
No kernel may reach another device: no remote copies, remote signals or barrier semaphores. Data moves between devices by JAX's collectives and lax.ppermute only.
A program may use at most 128 MiB of HBM per device.

```python
import math
import jax
import jax.numpy as jnp
from jax import lax

CH_DEV = 64
SAMPLES = 512
LAGS = 64
SECT_CH = 256
SECTIONS = 4


def draw_partners(key, part):
    order_key = jax.random.fold_in(key, 11)
    round_key = jax.random.fold_in(key, 23)
    circle = jax.random.permutation(order_key, SECTIONS).astype(jnp.int32)
    sections = jnp.arange(SECTIONS, dtype=jnp.int32)
    places = jnp.zeros((SECTIONS,), jnp.int32).at[circle].set(sections)
    rounds = jax.random.randint(round_key, (), 1, SECTIONS).astype(jnp.int32)
    after = circle[(places + rounds) % SECTIONS]
    before = circle[(places - rounds + SECTIONS) % SECTIONS]
    return jnp.stack([after, before], axis=1).astype(jnp.int32)


def block_levels(own_key, shape, pieces, least, largest):
    factor_of, own = 1.0, jax.random.fold_in(own_key, 6)
    for axis_at, parts in pieces:
        heights = jnp.exp(jax.random.uniform(jax.random.fold_in(own, axis_at), (parts,), jnp.float32, least / len(pieces), largest / len(pieces)))
        factor_of = factor_of * jnp.repeat(heights, shape[axis_at] // parts).reshape([-1 if axis == axis_at else 1 for axis in range(len(shape))])
    return factor_of


def centred(own_key, shape, deviation, most, cuts=(), kind=jnp.bfloat16):
    result = jax.random.normal(own_key, shape, jnp.float32) * deviation
    if len(cuts) > 0:
        result = block_levels(own_key, shape, cuts, -0.22, 0.18) * result
    return jnp.clip(result, min=-most, max=most).astype(kind)


def setup_inputs(seed: int = 0, part: int = 0) -> dict:
    key_list = jax.random.split(jax.random.key(seed), 4)
    own_keys = jax.random.split(jax.random.fold_in(key_list[3], part), 4)
    traces = centred(own_keys[0], (SECTIONS, SECT_CH, SAMPLES), 1.0, 6.0, ((0, 4), (1, 4)))
    positions = jax.vmap(lambda own: jax.random.permutation(own, SECT_CH))(jax.random.split(key_list[1], SECTIONS)).reshape((SECTIONS, SECT_CH)).astype(jnp.int32)
    partners = draw_partners(jax.random.fold_in(key_list[3], 71), part)
    return {"traces": traces, "positions": positions, "partners": partners}


def shifted(block):
    half = LAGS // 2
    width = block.shape[1]
    padded = jnp.pad(block, ((0, 0), (LAGS, LAGS)))
    return jnp.stack([padded[:, LAGS + half - lag_index:LAGS + half - lag_index + width] for lag_index in range(LAGS)], axis=1)

def section_terms(shift_x, places_x, other, places_other):
    count = shift_x.shape[0]
    flat = shift_x.reshape(count * LAGS, shift_x.shape[2])
    correlation = lax.dot_general(flat, other, (((1,), (1,)), ((), ())), precision=lax.Precision.HIGHEST, preferred_element_type=jnp.float32)
    correlation = correlation.reshape(count, LAGS, other.shape[0])
    root_mean = jnp.sqrt(lax.optimization_barrier(jnp.mean(correlation * correlation, axis=1)) + 1e-06)
    normed = correlation / root_mean[:, None, :]
    ahead = (places_other[None, :] >= places_x[:, None]).astype(jnp.float32)
    forward = lax.optimization_barrier(jnp.sum(normed * ahead[:, None, :], axis=2))
    backward = lax.optimization_barrier(jnp.sum(normed * (1.0 - ahead)[:, None, :], axis=2))
    return jnp.stack([forward, backward], axis=1)

def reference(traces, positions, partners):
    data = traces.astype(jnp.float32)
    blocks = SECT_CH // CH_DEV
    zero = jnp.zeros((), jnp.int32)

    def one_section(section):
        targets = [section, partners[section, 0], partners[section, 1]]

        def one_block(block):
            start = (block * CH_DEV).astype(jnp.int32)
            rows = lax.dynamic_slice(data, (section, start, zero), (1, CH_DEV, SAMPLES))[0]
            places = lax.dynamic_slice(positions, (section, start), (1, CH_DEV))[0]
            shift_x = shifted(rows)
            terms = [section_terms(shift_x, places, data[target], positions[target]) for target in targets]
            return jnp.stack(terms, axis=1)
        return lax.map(one_block, jnp.arange(blocks, dtype=jnp.int32))
    stacked = lax.map(one_section, jnp.arange(SECTIONS, dtype=jnp.int32))
    return (stacked * (1.0 / math.sqrt(SECT_CH))).reshape(SECTIONS, SECT_CH, 3, 2 * LAGS)
```

```python
import functools
import math

import jax
import jax.numpy as jnp
from jax import lax
from jax.experimental import pallas as pl
from jax.experimental.pallas import tpu as pltpu
from jax.sharding import PartitionSpec as P

LAGS = 64
HALF = LAGS // 2
LANES = 128
TILE = 256


def build_windows(x, t_ref):
    rows, width = x.shape
    lane = lax.broadcasted_iota(jnp.int32, (rows, width), 1)
    zero = jnp.zeros_like(x)
    for lag in range(LAGS):
        shift = HALF - lag
        start = (2 * (lag % HALF) + lag // HALF) * rows
        moved = x
        if shift != 0:
            inside = (lane < width - shift) if shift > 0 else (lane >= -shift)
            moved = jnp.where(inside, pltpu.roll(x, (-shift) % width, 1), zero)
        t_ref[pl.ds(start, rows), :] = moved


def stack_kernel(
    sel_ref, x_ref, g_ref, pos_ref, own_ref, o_ref, t_ref, c_ref, w_ref, acc_ref, *, blk, nblk, scale
):
    rows = x_ref.shape[0]
    build_windows(x_ref[...], t_ref)
    ncol = LAGS * rows // LANES
    own = own_ref[...]
    for k in range(3):
        q = sel_ref[k]
        acc_ref[...] = jnp.zeros_like(acc_ref)

        @pl.loop(0, nblk)
        def _(b):
            xq = g_ref[q, pl.ds(b * blk, blk), :]
            power = jnp.zeros((blk, LANES), jnp.float32)
            for n in range(LAGS * rows // TILE):
                cols = slice(n * TILE, (n + 1) * TILE)
                c = lax.dot_general(
                    xq,
                    t_ref[cols, :],
                    (((1,), (1,)), ((), ())),
                    preferred_element_type=jnp.float32,
                )
                c_ref[:, cols] = c
                for h in range(TILE // LANES):
                    part = c[:, h * LANES : (h + 1) * LANES]
                    power = power + part * part
            power = power + pltpu.roll(power, rows, 1)
            w = scale / jnp.sqrt(power * (1.0 / LAGS) + 1e-6)
            row = pos_ref[q, :, pl.ds(b * blk, blk)]
            column = jnp.transpose(jnp.broadcast_to(row, (8, blk)))[:, 0:1]
            ahead = column >= own
            w_ref[0] = jnp.where(ahead, w, 0.0)
            w_ref[1] = jnp.where(ahead, 0.0, w)
            for n in range(ncol):
                part = c_ref[:, n * LANES : (n + 1) * LANES]
                for side in range(2):
                    total = jnp.sum(part * w_ref[side], axis=0, keepdims=True)
                    acc_ref[pl.ds(side * ncol + n, 1), :] += total

        turned = jnp.transpose(acc_ref[...])
        o_ref[:, k, :] = jnp.concatenate(
            [turned[p * rows : (p + 1) * rows, s * ncol : (s + 1) * ncol] for s in range(2) for p in range(2)],
            axis=1,
        )


def stacks_of(sel, x, g, places, own):
    rows, width = x.shape
    sections, count, _ = g.shape
    ncol = LAGS * rows // LANES
    vmem = pl.BlockSpec(memory_space=pltpu.VMEM)
    return pl.pallas_call(
        functools.partial(stack_kernel, blk=TILE, nblk=count // TILE, scale=1.0 / math.sqrt(count)),
        out_shape=jax.ShapeDtypeStruct((rows, 3, 2 * LAGS), jnp.float32),
        in_specs=[pl.BlockSpec(memory_space=pltpu.SMEM)] + [vmem] * 4,
        out_specs=vmem,
        scratch_shapes=[
            pltpu.VMEM((LAGS * rows, width), jnp.bfloat16),
            pltpu.VMEM((TILE, LAGS * rows), jnp.float32),
            pltpu.VMEM((2, TILE, LANES), jnp.float32),
            pltpu.VMEM((2 * ncol, LANES), jnp.float32),
        ],
        compiler_params=pltpu.CompilerParams(vmem_limit_bytes=48 << 20),
    )(sel, x, g, places, own)


def flip(x, axis, bit):
    n = lax.axis_size(axis)
    return lax.ppermute(x, axis, [(d, d ^ bit) for d in range(n)])


def body(traces, positions, partners):
    x = traces[0]
    rows = x.shape[0]
    chans = lax.axis_size("chan")
    sections = lax.axis_size("sect")
    me = lax.axis_index("sect")
    chan = lax.axis_index("chan")
    targets = jnp.stack([me, partners[me, 0], partners[me, 1]])
    places = positions.astype(jnp.float32).reshape(sections, chans, rows)
    own = places[me, chan]
    own = jnp.concatenate([own, own])[None]
    if chans == 4 and sections == 4:
        pieces = [x] + [flip(x, "sect", k) for k in (1, 2, 3)]
        held = jnp.stack(pieces)[targets ^ me]
        held = jnp.stack([held, flip(held, "chan", 2)], axis=1)
        held = jnp.concatenate([held, flip(held, "chan", 1)], axis=1)
        order = chan ^ jnp.array([0, 2, 1, 3], jnp.int32)
        places = places[targets][:, order]
        whole = held.reshape(3, chans * rows, x.shape[1])
        sel = jnp.arange(3, dtype=jnp.int32)
    else:
        whole = lax.all_gather(x, "chan", axis=0, tiled=True)
        whole = lax.all_gather(whole[None], "sect", axis=0, tiled=True)
        sel = targets
    places = places.reshape(places.shape[0], 1, chans * rows)
    return stacks_of(sel, x, whole, places, own)[None]


def solution(mesh):
    in_specs = (P(("days", "sect"), "chan", None), P(), P())
    out_specs = P(("days", "sect"), "chan", None, None)
    return jax.shard_map(body, mesh=mesh, in_specs=in_specs, out_specs=out_specs, check_vma=False)
```

```python
import functools
import math

import jax
import jax.numpy as jnp
from jax import lax
from jax.experimental import pallas as pl
from jax.experimental.pallas import tpu as pltpu
from jax.sharding import PartitionSpec as P

LAGS = 64
HALF = LAGS // 2
LANES = 128
TILE = 256
VMEM = pl.BlockSpec(memory_space=pltpu.VMEM)
SMEM = pl.BlockSpec(memory_space=pltpu.SMEM)


def build_windows(x, t_ref):
    rows, width = x.shape
    lane = lax.broadcasted_iota(jnp.int32, (rows, width), 1)
    zero = jnp.zeros_like(x)
    for lag in range(LAGS):
        shift = HALF - lag
        start = (2 * (lag % HALF) + lag // HALF) * rows
        moved = x
        if shift != 0:
            inside = (lane < width - shift) if shift > 0 else (lane >= -shift)
            moved = jnp.where(inside, pltpu.roll(x, (-shift) % width, 1), zero)
        t_ref[pl.ds(start, rows), :] = moved


def products(xq, t_ref, c_ref):
    power = jnp.zeros((xq.shape[0], LANES), jnp.float32)
    for n in range(t_ref.shape[0] // TILE):
        cols = slice(n * TILE, (n + 1) * TILE)
        c = lax.dot_general(
            xq, t_ref[cols, :], (((1,), (1,)), ((), ())), preferred_element_type=jnp.float32
        )
        c_ref[:, cols] = c
        for h in range(TILE // LANES):
            part = c[:, h * LANES : (h + 1) * LANES]
            power = power + part * part
    return power + pltpu.roll(power, LANES // 2, 1)


def column_of(row):
    return jnp.transpose(jnp.broadcast_to(row, (8, row.shape[1])))[:, 0:1]


def weigh(power, columns, own, w_ref, scale):
    w = scale / jnp.sqrt(power * (1.0 / LAGS) + 1e-6)
    ahead = columns >= own
    w_ref[0] = jnp.where(ahead, w, 0.0)
    w_ref[1] = jnp.where(ahead, 0.0, w)


def side_sums(c_ref, w_ref, low, high, put):
    ncol = c_ref.shape[1] // LANES
    for n in range(ncol):
        part = c_ref[low:high, n * LANES : (n + 1) * LANES]
        for side in range(2):
            put(side * ncol + n, jnp.sum(part * w_ref[side, low:high], axis=0, keepdims=True))


def by_channel(sums, rows):
    ncol = sums.shape[0] // 2
    turned = jnp.transpose(sums)
    return jnp.concatenate(
        [
            turned[p * rows : (p + 1) * rows, s * ncol : (s + 1) * ncol]
            for s in range(2)
            for p in range(2)
        ],
        axis=1,
    )


def stack_kernel(
    sel_ref, x_ref, g_ref, pos_ref, own_ref, o_ref, t_ref, c_ref, w_ref, acc_ref, *, nblk, scale
):
    rows = x_ref.shape[0]
    build_windows(x_ref[...], t_ref)
    own = own_ref[...]
    for k in range(3):
        q = sel_ref[k]
        acc_ref[...] = jnp.zeros_like(acc_ref)

        @pl.loop(0, nblk)
        def _(b):
            power = products(g_ref[q, pl.ds(b * TILE, TILE), :], t_ref, c_ref)
            columns = column_of(pos_ref[q, :, pl.ds(b * TILE, TILE)])
            weigh(power, columns, own, w_ref, scale)

            def put(row, value):
                acc_ref[pl.ds(row, 1), :] += value

            side_sums(c_ref, w_ref, 0, TILE, put)

        o_ref[:, k, :] = by_channel(acc_ref[...], rows)


def scratch(rows, width):
    return [
        pltpu.VMEM((LAGS * rows, width), jnp.bfloat16),
        pltpu.VMEM((TILE, LAGS * rows), jnp.float32),
        pltpu.VMEM((2, TILE, LANES), jnp.float32),
    ]


def sums_shape(rows, count=None):
    shape = (2 * LAGS * rows // LANES, LANES)
    return shape if count is None else (count,) + shape


PARAMS = pltpu.CompilerParams(vmem_limit_bytes=48 << 20)


def stacks_anywhere(x, traces, positions, targets, me, chan):
    rows, width = x.shape
    chans, sections = lax.axis_size("chan"), lax.axis_size("sect")
    count = chans * rows
    whole = lax.all_gather(x, "chan", axis=0, tiled=True)
    whole = lax.all_gather(whole[None], "sect", axis=0, tiled=True)
    places = positions.astype(jnp.float32)
    own = lax.dynamic_slice(places, (me, chan * rows), (1, rows))
    own = jnp.concatenate([own, own], axis=1)
    return pl.pallas_call(
        functools.partial(stack_kernel, nblk=count // TILE, scale=1.0 / math.sqrt(count)),
        out_shape=jax.ShapeDtypeStruct((rows, 3, 2 * LAGS), jnp.float32),
        in_specs=[SMEM] + [VMEM] * 4,
        out_specs=VMEM,
        scratch_shapes=scratch(rows, width) + [pltpu.VMEM(sums_shape(rows), jnp.float32)],
        compiler_params=PARAMS,
    )(targets, x, whole, places.reshape(sections, 1, count), own)


def place_row(pos_ref, q):
    every = pos_ref[...].astype(jnp.float32)
    at = lax.broadcasted_iota(jnp.int32, every.shape, 0)
    return jnp.sum(jnp.where(at == q, every, 0.0), axis=0, keepdims=True)


def half_row(row, half):
    return jnp.where(half == 0, row[:, :LANES], row[:, LANES:])


def twice(row, core):
    turned = pltpu.roll(row, LANES // 2, 1)
    low = lax.broadcasted_iota(jnp.int32, row.shape, 1) // (LANES // 2)
    return jnp.where(low == core, row, turned)


def where_am_i():
    me, chan = lax.axis_index("sect"), lax.axis_index("chan")
    return me, chan // 2, chan % 2


def own_kernel(x_ref, co_ref, yo_ref, cyo_ref, pos_ref, o_ref, t_ref, c_ref, w_ref, xs_ref, *, scale):
    me, half, core = where_am_i()
    rows = x_ref.shape[0]
    for flipped, ref in ((0, x_ref), (1, co_ref), (2, yo_ref), (3, cyo_ref)):
        at = ((2 * half + core) ^ flipped) * rows
        xs_ref[pl.ds(pl.multiple_of(at, rows), rows), :] = ref[...]
    build_windows(x_ref[...], t_ref)
    power = products(xs_ref[...], t_ref, c_ref)
    row = place_row(pos_ref, me)
    weigh(power, column_of(row), twice(half_row(row, half), core), w_ref, scale)

    def put(at, value):
        o_ref[at : at + 1, :] = value

    side_sums(c_ref, w_ref, 0, 4 * rows, put)


def pair_kernel(*refs, scale, across):
    partners_ref, x_ref = refs[:2]
    mine, peers = refs[2:5], refs[5:8]
    pos_ref, o_ref, t_ref, c_ref, w_ref, xs_ref = refs[8:]
    me, half, core = where_am_i()
    rows = x_ref.shape[0]
    whose = [partners_ref[k, me] for k in range(2)]
    for k in range(2):
        low = pl.multiple_of((2 * k + core) * rows, rows)
        high = pl.multiple_of((2 * k + 1 - core) * rows, rows)
        for away in range(3):

            @pl.when((whose[k] ^ me) == away + 1)
            def _():
                xs_ref[pl.ds(low, rows), :] = mine[away][...]
                xs_ref[pl.ds(high, rows), :] = peers[away][...]

    build_windows(x_ref[...], t_ref)
    power = products(xs_ref[...], t_ref, c_ref)
    columns = column_of(jnp.concatenate([half_row(place_row(pos_ref, q), half) for q in whose], axis=1))
    ours = half_row(place_row(pos_ref, me), 1 - half if across else half)
    weigh(power, columns, twice(ours, core), w_ref, scale)
    for k in range(2):

        def put(at, value):
            o_ref[k, at : at + 1, :] = value

        side_sums(c_ref, w_ref, 2 * rows * k, 2 * rows * (k + 1), put)


def join_kernel(own_ref, here_ref, there_ref, o_ref):
    rows = o_ref.shape[1]
    o_ref[0] = by_channel(own_ref[...], rows)
    for k in range(2):
        o_ref[1 + k] = by_channel(here_ref[k] + there_ref[k], rows)


def send(x, to):
    chans, sections = lax.axis_size("chan"), lax.axis_size("sect")
    pairs = []
    for c in range(chans):
        for s in range(sections):
            c2, s2 = to(c, s)
            pairs.append((c * sections + s, c2 * sections + s2))
    return lax.ppermute(x, ("chan", "sect"), pairs)


def stacks_by_flips(x, positions, partners):
    rows, width = x.shape
    scale = 1.0 / math.sqrt(4 * rows)
    z2 = send(x, lambda c, s: (c, s ^ 2))
    z3 = send(x, lambda c, s: (c, s ^ 3))
    z1 = send(x, lambda c, s: (c, s ^ 1))
    yo = send(x, lambda c, s: (c ^ 2, s))
    co = send(x, lambda c, s: (c ^ 1, s))
    co, yo, z1, z3, z2 = lax.optimization_barrier((co, yo, z1, z3, z2))
    cyo = send(yo, lambda c, s: (c ^ 1, s))
    cz1 = send(z1, lambda c, s: (c ^ 1, s))
    space = scratch(rows, width) + [pltpu.VMEM((4 * rows, width), jnp.bfloat16)]
    common = dict(out_specs=VMEM, compiler_params=PARAMS)
    own = pl.pallas_call(
        functools.partial(own_kernel, scale=scale),
        out_shape=jax.ShapeDtypeStruct(sums_shape(rows), jnp.float32),
        in_specs=[VMEM] * 5,
        scratch_shapes=space,
        **common,
    )(x, co, yo, cyo, positions)
    cz2 = send(z2, lambda c, s: (c ^ 1, s))
    cz3 = send(z3, lambda c, s: (c ^ 1, s))

    def pairs_of(source, across):
        return pl.pallas_call(
            functools.partial(pair_kernel, scale=scale, across=across),
            out_shape=jax.ShapeDtypeStruct(sums_shape(rows, 2), jnp.float32),
            in_specs=[SMEM] + [VMEM] * 8,
            scratch_shapes=space,
            **common,
        )(jnp.transpose(partners), source, z1, z2, z3, cz1, cz2, cz3, positions)

    there = send(pairs_of(yo, True), lambda c, s: (c ^ 2, s))
    here = pairs_of(x, False)
    stacks = pl.pallas_call(
        join_kernel,
        out_shape=jax.ShapeDtypeStruct((3, rows, 2 * LAGS), jnp.float32),
        in_specs=[VMEM] * 3,
        **common,
    )(own, here, there)
    return jnp.transpose(stacks, (1, 0, 2))


def body(traces, positions, partners):
    x = traces[0]
    me = lax.axis_index("sect")
    chan = lax.axis_index("chan")
    if lax.axis_size("chan") == 4 and lax.axis_size("sect") == 4:
        return stacks_by_flips(x, positions, partners)[None]
    targets = jnp.stack([me, partners[me, 0], partners[me, 1]])
    return stacks_anywhere(x, traces, positions, targets, me, chan)[None]


def solution(mesh):
    in_specs = (P(("days", "sect"), "chan", None), P(), P())
    out_specs = P(("days", "sect"), "chan", None, None)
    return jax.shard_map(body, mesh=mesh, in_specs=in_specs, out_specs=out_specs, check_vma=False)
```

```python
import functools
import math

import jax
import jax.numpy as jnp
from jax import lax
from jax.experimental import pallas as pl
from jax.experimental.pallas import tpu as pltpu
from jax.sharding import PartitionSpec as P

LAGS = 64
HALF = LAGS // 2
LANES = 128
TILE = 256
VMEM = pl.BlockSpec(memory_space=pltpu.VMEM)
SMEM = pl.BlockSpec(memory_space=pltpu.SMEM)


def build_windows(x, t_ref):
    rows, width = x.shape
    lane = lax.broadcasted_iota(jnp.int32, (rows, width), 1)
    zero = jnp.zeros_like(x)
    for lag in range(LAGS):
        shift = HALF - lag
        start = (2 * (lag % HALF) + lag // HALF) * rows
        moved = x
        if shift != 0:
            inside = (lane < width - shift) if shift > 0 else (lane >= -shift)
            moved = jnp.where(inside, pltpu.roll(x, (-shift) % width, 1), zero)
        t_ref[pl.ds(start, rows), :] = moved


def products(xq, t_ref, c_ref):
    power = jnp.zeros((xq.shape[0], LANES), jnp.float32)
    for n in range(t_ref.shape[0] // TILE):
        cols = slice(n * TILE, (n + 1) * TILE)
        c = lax.dot_general(
            xq, t_ref[cols, :], (((1,), (1,)), ((), ())), preferred_element_type=jnp.float32
        )
        c_ref[:, cols] = c
        for h in range(TILE // LANES):
            part = c[:, h * LANES : (h + 1) * LANES]
            power = power + part * part
    return power + pltpu.roll(power, LANES // 2, 1)


def column_of(row):
    return jnp.transpose(jnp.broadcast_to(row, (8, row.shape[1])))[:, 0:1]


def weigh(power, columns, own, w_ref, scale):
    w = scale / jnp.sqrt(power * (1.0 / LAGS) + 1e-6)
    ahead = columns >= own
    w_ref[0] = jnp.where(ahead, w, 0.0)
    w_ref[1] = jnp.where(ahead, 0.0, w)


def side_sums(c_ref, w_ref, low, high, put):
    ncol = c_ref.shape[1] // LANES
    for n in range(ncol):
        part = c_ref[low:high, n * LANES : (n + 1) * LANES]
        for side in range(2):
            put(side * ncol + n, jnp.sum(part * w_ref[side, low:high], axis=0, keepdims=True))


def by_channel(sums, rows):
    ncol = sums.shape[0] // 2
    turned = jnp.transpose(sums)
    return jnp.concatenate(
        [
            turned[p * rows : (p + 1) * rows, s * ncol : (s + 1) * ncol]
            for s in range(2)
            for p in range(2)
        ],
        axis=1,
    )


def stack_kernel(
    sel_ref, x_ref, g_ref, pos_ref, own_ref, o_ref, t_ref, c_ref, w_ref, acc_ref, *, nblk, scale
):
    rows = x_ref.shape[0]
    build_windows(x_ref[...], t_ref)
    own = own_ref[...]
    for k in range(3):
        q = sel_ref[k]
        acc_ref[...] = jnp.zeros_like(acc_ref)

        @pl.loop(0, nblk)
        def _(b):
            power = products(g_ref[q, pl.ds(b * TILE, TILE), :], t_ref, c_ref)
            columns = column_of(pos_ref[q, :, pl.ds(b * TILE, TILE)])
            weigh(power, columns, own, w_ref, scale)

            def put(row, value):
                acc_ref[pl.ds(row, 1), :] += value

            side_sums(c_ref, w_ref, 0, TILE, put)

        o_ref[:, k, :] = by_channel(acc_ref[...], rows)


def scratch(rows, width):
    return [
        pltpu.VMEM((LAGS * rows, width), jnp.bfloat16),
        pltpu.VMEM((TILE, LAGS * rows), jnp.float32),
        pltpu.VMEM((2, TILE, LANES), jnp.float32),
    ]


def sums_shape(rows, count=None):
    shape = (2 * LAGS * rows // LANES, LANES)
    return shape if count is None else (count,) + shape


PARAMS = pltpu.CompilerParams(vmem_limit_bytes=48 << 20)


def stacks_anywhere(x, traces, positions, targets, me, chan):
    rows, width = x.shape
    chans, sections = lax.axis_size("chan"), lax.axis_size("sect")
    count = chans * rows
    whole = lax.all_gather(x, "chan", axis=0, tiled=True)
    whole = lax.all_gather(whole[None], "sect", axis=0, tiled=True)
    places = positions.astype(jnp.float32)
    own = lax.dynamic_slice(places, (me, chan * rows), (1, rows))
    own = jnp.concatenate([own, own], axis=1)
    return pl.pallas_call(
        functools.partial(stack_kernel, nblk=count // TILE, scale=1.0 / math.sqrt(count)),
        out_shape=jax.ShapeDtypeStruct((rows, 3, 2 * LAGS), jnp.float32),
        in_specs=[SMEM] + [VMEM] * 4,
        out_specs=VMEM,
        scratch_shapes=scratch(rows, width) + [pltpu.VMEM(sums_shape(rows), jnp.float32)],
        compiler_params=PARAMS,
    )(targets, x, whole, places.reshape(sections, 1, count), own)


def place_row(pos_ref, q):
    every = pos_ref[...].astype(jnp.float32)
    at = lax.broadcasted_iota(jnp.int32, every.shape, 0)
    return jnp.sum(jnp.where(at == q, every, 0.0), axis=0, keepdims=True)


def half_row(row, half):
    return jnp.where(half == 0, row[:, :LANES], row[:, LANES:])


def twice(row, core):
    turned = pltpu.roll(row, LANES // 2, 1)
    low = lax.broadcasted_iota(jnp.int32, row.shape, 1) // (LANES // 2)
    return jnp.where(low == core, row, turned)


def where_am_i():
    me, chan = lax.axis_index("sect"), lax.axis_index("chan")
    return me, chan // 2, chan % 2


def places_kernel(partners_ref, x_ref, pos_ref, xv_ref, rows_ref, cols_ref):
    me, half, core = where_am_i()
    xv_ref[...] = x_ref[...]
    row = place_row(pos_ref, me)
    rows_ref[0:1, :] = twice(half_row(row, half), core)
    rows_ref[1:2, :] = twice(half_row(row, 1 - half), core)
    whose = [partners_ref[k, me] for k in range(2)]
    for k in range(2):
        rows_ref[2 + k : 3 + k, :] = jnp.full((1, LANES), whose[k] ^ me, jnp.int32).astype(jnp.float32)
    near = jnp.concatenate([half_row(place_row(pos_ref, q), half) for q in whose], axis=1)
    cols_ref[0] = jnp.broadcast_to(column_of(near), cols_ref.shape[1:])
    cols_ref[1] = jnp.broadcast_to(column_of(row), cols_ref.shape[1:])


def gather_pairs(mine, peers, rows_ref, xs_ref, rows):
    core = lax.axis_index("chan") % 2
    for k in range(2):
        away = rows_ref[2 + k : 3 + k, :]
        picks = [(away == 1.0 + z).astype(jnp.bfloat16) for z in range(3)]
        for w in range(xs_ref.shape[1] // LANES):
            cut = slice(w * LANES, (w + 1) * LANES)
            own = sum(ref[:, cut] * pick for ref, pick in zip(mine, picks))
            peer = sum(peers[z * rows : (z + 1) * rows, cut] * pick for z, pick in enumerate(picks))
            low = pl.multiple_of((2 * k + core) * rows, rows)
            high = pl.multiple_of((2 * k + 1 - core) * rows, rows)
            xs_ref[pl.ds(low, rows), cut] = own
            xs_ref[pl.ds(high, rows), cut] = peer


def pair_sums(xs_ref, t_ref, c_ref, w_ref, rows_ref, cols_ref, line, o_ref, rows, scale):
    power = products(xs_ref[...], t_ref, c_ref)
    weigh(power, cols_ref[0], rows_ref[line : line + 1, :], w_ref, scale)
    for k in range(2):

        def put(at, value):
            o_ref[k, at : at + 1, :] = value

        side_sums(c_ref, w_ref, 2 * rows * k, 2 * rows * (k + 1), put)


def across_kernel(
    yo_ref, z1_ref, z2_ref, z3_ref, cz_ref, rows_ref, cols_ref, o_ref, t_ref, c_ref, w_ref, xs_ref, *, scale
):
    rows = yo_ref.shape[0]
    gather_pairs((z1_ref, z2_ref, z3_ref), cz_ref, rows_ref, xs_ref, rows)
    build_windows(yo_ref[...], t_ref)
    pair_sums(xs_ref, t_ref, c_ref, w_ref, rows_ref, cols_ref, 1, o_ref, rows, scale)


def here_kernel(
    x_ref, co_ref, yo_ref, cyo_ref, z1_ref, z2_ref, z3_ref, cz_ref, rows_ref, cols_ref, o_ref, own_ref, t_ref, c_ref, w_ref, xs_ref, *, scale
):
    me, half, core = where_am_i()
    rows = x_ref.shape[0]
    build_windows(x_ref[...], t_ref)
    gather_pairs((z1_ref, z2_ref, z3_ref), cz_ref, rows_ref, xs_ref, rows)
    pair_sums(xs_ref, t_ref, c_ref, w_ref, rows_ref, cols_ref, 0, o_ref, rows, scale)
    for flipped, ref in ((0, x_ref), (1, co_ref), (2, yo_ref), (3, cyo_ref)):
        at = ((2 * half + core) ^ flipped) * rows
        xs_ref[pl.ds(pl.multiple_of(at, rows), rows), :] = ref[...]
    power = products(xs_ref[...], t_ref, c_ref)
    weigh(power, cols_ref[1], rows_ref[0:1, :], w_ref, scale)

    def put(at, value):
        own_ref[at : at + 1, :] = value

    side_sums(c_ref, w_ref, 0, 4 * rows, put)


def join_kernel(own_ref, here_ref, there_ref, o_ref):
    rows = o_ref.shape[1]
    o_ref[0] = by_channel(own_ref[...], rows)
    for k in range(2):
        o_ref[1 + k] = by_channel(here_ref[k] + there_ref[k], rows)


def send(x, to):
    chans, sections = lax.axis_size("chan"), lax.axis_size("sect")
    pairs = []
    for c in range(chans):
        for s in range(sections):
            c2, s2 = to(c, s)
            pairs.append((c * sections + s, c2 * sections + s2))
    return lax.ppermute(x, ("chan", "sect"), pairs)


def stacks_by_flips(x, positions, partners):
    rows, width = x.shape
    scale = 1.0 / math.sqrt(4 * rows)
    f32 = jnp.float32
    xv, lines, columns = pl.pallas_call(
        places_kernel,
        out_shape=[
            jax.ShapeDtypeStruct(x.shape, x.dtype),
            jax.ShapeDtypeStruct((8, LANES), f32),
            jax.ShapeDtypeStruct((2, 4 * rows, LANES), f32),
        ],
        in_specs=[SMEM] + [VMEM] * 2,
        out_specs=[VMEM] * 3,
        compiler_params=PARAMS,
    )(jnp.transpose(partners), x, positions)
    z1, z2, z3 = [send(x, lambda c, s: (c, s ^ k)) for k in (1, 2, 3)]
    co, yo = [send(x, lambda c, s: (c ^ k, s)) for k in (1, 2)]
    xv, lines, columns, z2, z3, z1, yo, co = lax.optimization_barrier((xv, lines, columns, z2, z3, z1, yo, co))
    cz = send(jnp.concatenate([z1, z2, z3]), lambda c, s: (c ^ 1, s))
    cyo = send(yo, lambda c, s: (c ^ 1, s))
    space = scratch(rows, width) + [pltpu.VMEM((4 * rows, width), x.dtype)]
    sums = jax.ShapeDtypeStruct(sums_shape(rows), f32)
    pair = jax.ShapeDtypeStruct(sums_shape(rows, 2), f32)
    across = pl.pallas_call(
        functools.partial(across_kernel, scale=scale),
        out_shape=pair,
        in_specs=[VMEM] * 7,
        out_specs=VMEM,
        scratch_shapes=space,
        compiler_params=PARAMS,
    )(yo, z1, z2, z3, cz, lines, columns)
    there = send(across, lambda c, s: (c ^ 2, s))
    here, own = pl.pallas_call(
        functools.partial(here_kernel, scale=scale),
        out_shape=[pair, sums],
        in_specs=[VMEM] * 10,
        out_specs=[VMEM] * 2,
        scratch_shapes=space,
        compiler_params=PARAMS,
    )(xv, co, yo, cyo, z1, z2, z3, cz, lines, columns)
    stacks = pl.pallas_call(
        join_kernel,
        out_shape=jax.ShapeDtypeStruct((3, rows, 2 * LAGS), f32),
        in_specs=[VMEM] * 3,
        out_specs=VMEM,
        compiler_params=PARAMS,
    )(own, here, there)
    return jnp.transpose(stacks, (1, 0, 2))


def body(traces, positions, partners):
    x = traces[0]
    me = lax.axis_index("sect")
    chan = lax.axis_index("chan")
    if lax.axis_size("chan") == 4 and lax.axis_size("sect") == 4:
        return stacks_by_flips(x, positions, partners)[None]
    targets = jnp.stack([me, partners[me, 0], partners[me, 1]])
    return stacks_anywhere(x, traces, positions, targets, me, chan)[None]


def solution(mesh):
    in_specs = (P(("days", "sect"), "chan", None), P(), P())
    out_specs = P(("days", "sect"), "chan", None, None)
    return jax.shard_map(body, mesh=mesh, in_specs=in_specs, out_specs=out_specs, check_vma=False)
```

```python
import functools
import math

import jax
import jax.numpy as jnp
from jax import lax
from jax.experimental import pallas as pl
from jax.experimental.pallas import tpu as pltpu
from jax.sharding import PartitionSpec as P

LAGS = 64
HALF = LAGS // 2
LANES = 128
TILE = 256
VMEM = pl.BlockSpec(memory_space=pltpu.VMEM)
SMEM = pl.BlockSpec(memory_space=pltpu.SMEM)
HBM = pl.BlockSpec(memory_space=pltpu.MemorySpace.HBM)


def build_windows(x, t_ref):
    rows, width = x.shape
    lane = lax.broadcasted_iota(jnp.int32, (rows, width), 1)
    zero = jnp.zeros_like(x)
    for lag in range(LAGS):
        shift = HALF - lag
        start = (2 * (lag % HALF) + lag // HALF) * rows
        moved = x
        if shift != 0:
            inside = (lane < width - shift) if shift > 0 else (lane >= -shift)
            moved = jnp.where(inside, pltpu.roll(x, (-shift) % width, 1), zero)
        t_ref[pl.ds(start, rows), :] = moved


def products(xq, t_ref, c_ref):
    power = jnp.zeros((xq.shape[0], LANES), jnp.float32)
    for n in range(t_ref.shape[0] // TILE):
        cols = slice(n * TILE, (n + 1) * TILE)
        c = lax.dot_general(
            xq, t_ref[cols, :], (((1,), (1,)), ((), ())), preferred_element_type=jnp.float32
        )
        c_ref[:, cols] = c
        for h in range(TILE // LANES):
            part = c[:, h * LANES : (h + 1) * LANES]
            power = power + part * part
    return power + pltpu.roll(power, LANES // 2, 1)


def column_of(row):
    return jnp.transpose(jnp.broadcast_to(row, (8, row.shape[1])))[:, 0:1]


def weigh(power, columns, own, w_ref, scale):
    w = scale * lax.rsqrt(power * (1.0 / LAGS) + 1e-6)
    ahead = columns >= own
    w_ref[0] = jnp.where(ahead, w, 0.0)
    w_ref[1] = jnp.where(ahead, 0.0, w)


def side_sums(c_ref, w_ref, low, high, put):
    ncol = c_ref.shape[1] // LANES
    for n in range(ncol):
        part = c_ref[low:high, n * LANES : (n + 1) * LANES]
        for side in range(2):
            put(side * ncol + n, jnp.sum(part * w_ref[side, low:high], axis=0, keepdims=True))


def by_channel(sums, rows):
    ncol = sums.shape[0] // 2
    turned = jnp.transpose(sums)
    return jnp.concatenate(
        [
            turned[p * rows : (p + 1) * rows, s * ncol : (s + 1) * ncol]
            for s in range(2)
            for p in range(2)
        ],
        axis=1,
    )


def stack_kernel(
    sel_ref, x_ref, g_ref, pos_ref, own_ref, o_ref, t_ref, c_ref, w_ref, acc_ref, *, nblk, scale
):
    rows = x_ref.shape[0]
    build_windows(x_ref[...], t_ref)
    own = own_ref[...]
    for k in range(3):
        q = sel_ref[k]
        acc_ref[...] = jnp.zeros_like(acc_ref)

        @pl.loop(0, nblk)
        def _(b):
            power = products(g_ref[q, pl.ds(b * TILE, TILE), :], t_ref, c_ref)
            columns = column_of(pos_ref[q, :, pl.ds(b * TILE, TILE)])
            weigh(power, columns, own, w_ref, scale)

            def put(row, value):
                acc_ref[pl.ds(row, 1), :] += value

            side_sums(c_ref, w_ref, 0, TILE, put)

        o_ref[:, k, :] = by_channel(acc_ref[...], rows)


def scratch(rows, width):
    return [
        pltpu.VMEM((LAGS * rows, width), jnp.bfloat16),
        pltpu.VMEM((TILE, LAGS * rows), jnp.float32),
        pltpu.VMEM((2, TILE, LANES), jnp.float32),
    ]


def sums_shape(rows, count=None):
    shape = (2 * LAGS * rows // LANES, LANES)
    return shape if count is None else (count,) + shape


PARAMS = pltpu.CompilerParams(vmem_limit_bytes=48 << 20)


def stacks_anywhere(x, traces, positions, targets, me, chan):
    rows, width = x.shape
    chans, sections = lax.axis_size("chan"), lax.axis_size("sect")
    count = chans * rows
    whole = lax.all_gather(x, "chan", axis=0, tiled=True)
    whole = lax.all_gather(whole[None], "sect", axis=0, tiled=True)
    places = positions.astype(jnp.float32)
    own = lax.dynamic_slice(places, (me, chan * rows), (1, rows))
    own = jnp.concatenate([own, own], axis=1)
    return pl.pallas_call(
        functools.partial(stack_kernel, nblk=count // TILE, scale=1.0 / math.sqrt(count)),
        out_shape=jax.ShapeDtypeStruct((rows, 3, 2 * LAGS), jnp.float32),
        in_specs=[SMEM] + [VMEM] * 4,
        out_specs=VMEM,
        scratch_shapes=scratch(rows, width) + [pltpu.VMEM(sums_shape(rows), jnp.float32)],
        compiler_params=PARAMS,
    )(targets, x, whole, places.reshape(sections, 1, count), own)


def place_row(pos_ref, q):
    every = pos_ref[...].astype(jnp.float32)
    at = lax.broadcasted_iota(jnp.int32, every.shape, 0)
    return jnp.sum(jnp.where(at == q, every, 0.0), axis=0, keepdims=True)


def half_row(row, half):
    return jnp.where(half == 0, row[:, :LANES], row[:, LANES:])


def twice(row, core):
    turned = pltpu.roll(row, LANES // 2, 1)
    low = lax.broadcasted_iota(jnp.int32, row.shape, 1) // (LANES // 2)
    return jnp.where(low == core, row, turned)


def where_am_i():
    me, chan = lax.axis_index("sect"), lax.axis_index("chan")
    return me, chan // 2, chan % 2


def places_kernel(partners_ref, x_ref, pos_ref, xv_ref, rows_ref, cols_ref, places_ref, sems):
    me, half, core = where_am_i()
    get_x = pltpu.make_async_copy(x_ref, xv_ref, sems.at[0])
    get_places = pltpu.make_async_copy(pos_ref, places_ref, sems.at[1])
    get_x.start()
    get_places.start()
    get_places.wait()
    row = place_row(places_ref, me)
    rows_ref[0:1, :] = twice(half_row(row, half), core)
    rows_ref[1:2, :] = twice(half_row(row, 1 - half), core)
    whose = [partners_ref[k, me] for k in range(2)]
    for k in range(2):
        rows_ref[2 + k : 3 + k, :] = jnp.full((1, LANES), whose[k] ^ me, jnp.int32).astype(jnp.float32)
    near = jnp.concatenate([half_row(place_row(places_ref, q), half) for q in whose], axis=1)
    cols_ref[0] = jnp.broadcast_to(column_of(near), cols_ref.shape[1:])
    cols_ref[1] = jnp.broadcast_to(column_of(row), cols_ref.shape[1:])
    get_x.wait()


def gather_pairs(mine, peers, rows_ref, xs_ref, rows):
    core = lax.axis_index("chan") % 2
    for k in range(2):
        away = rows_ref[2 + k : 3 + k, :]
        picks = [(away == 1.0 + z).astype(jnp.bfloat16) for z in range(3)]
        for w in range(xs_ref.shape[1] // LANES):
            cut = slice(w * LANES, (w + 1) * LANES)
            own = sum(ref[:, cut] * pick for ref, pick in zip(mine, picks))
            peer = sum(peers[z * rows : (z + 1) * rows, cut] * pick for z, pick in enumerate(picks))
            low = pl.multiple_of((2 * k + core) * rows, rows)
            high = pl.multiple_of((2 * k + 1 - core) * rows, rows)
            xs_ref[pl.ds(low, rows), cut] = own
            xs_ref[pl.ds(high, rows), cut] = peer


def pair_sums(xs_ref, t_ref, c_ref, w_ref, rows_ref, cols_ref, line, o_ref, rows, scale):
    power = products(xs_ref[...], t_ref, c_ref)
    weigh(power, cols_ref[0], rows_ref[line : line + 1, :], w_ref, scale)
    for k in range(2):

        def put(at, value):
            o_ref[k, at : at + 1, :] = value

        side_sums(c_ref, w_ref, 2 * rows * k, 2 * rows * (k + 1), put)


def across_kernel(
    yo_ref, z1_ref, z2_ref, z3_ref, cz_ref, rows_ref, cols_ref, o_ref, t_ref, c_ref, w_ref, xs_ref, *, scale
):
    rows = yo_ref.shape[0]
    gather_pairs((z1_ref, z2_ref, z3_ref), cz_ref, rows_ref, xs_ref, rows)
    build_windows(yo_ref[...], t_ref)
    pair_sums(xs_ref, t_ref, c_ref, w_ref, rows_ref, cols_ref, 1, o_ref, rows, scale)


def here_kernel(
    x_ref, co_ref, yo_ref, cyo_ref, z1_ref, z2_ref, z3_ref, cz_ref, rows_ref, cols_ref, o_ref, own_ref, t_ref, c_ref, w_ref, xs_ref, *, scale
):
    me, half, core = where_am_i()
    rows = x_ref.shape[0]
    build_windows(x_ref[...], t_ref)
    gather_pairs((z1_ref, z2_ref, z3_ref), cz_ref, rows_ref, xs_ref, rows)
    pair_sums(xs_ref, t_ref, c_ref, w_ref, rows_ref, cols_ref, 0, o_ref, rows, scale)
    for flipped, ref in ((0, x_ref), (1, co_ref), (2, yo_ref), (3, cyo_ref)):
        at = ((2 * half + core) ^ flipped) * rows
        xs_ref[pl.ds(pl.multiple_of(at, rows), rows), :] = ref[...]
    power = products(xs_ref[...], t_ref, c_ref)
    weigh(power, cols_ref[1], rows_ref[0:1, :], w_ref, scale)

    def put(at, value):
        own_ref[at : at + 1, :] = value

    side_sums(c_ref, w_ref, 0, 4 * rows, put)


def join_kernel(own_ref, here_ref, there_ref, o_ref):
    rows = o_ref.shape[1]
    o_ref[0] = by_channel(own_ref[...], rows)
    for k in range(2):
        o_ref[1 + k] = by_channel(here_ref[k] + there_ref[k], rows)


def send(x, to):
    chans, sections = lax.axis_size("chan"), lax.axis_size("sect")
    pairs = []
    for c in range(chans):
        for s in range(sections):
            c2, s2 = to(c, s)
            pairs.append((c * sections + s, c2 * sections + s2))
    return lax.ppermute(x, ("chan", "sect"), pairs)


def stacks_by_flips(x, positions, partners):
    rows, width = x.shape
    scale = 1.0 / math.sqrt(4 * rows)
    f32 = jnp.float32
    xv, lines, columns = pl.pallas_call(
        places_kernel,
        out_shape=[
            jax.ShapeDtypeStruct(x.shape, x.dtype),
            jax.ShapeDtypeStruct((8, LANES), f32),
            jax.ShapeDtypeStruct((2, 4 * rows, LANES), f32),
        ],
        in_specs=[SMEM, HBM, HBM],
        out_specs=[VMEM] * 3,
        scratch_shapes=[pltpu.VMEM(positions.shape, positions.dtype), pltpu.SemaphoreType.DMA((2,))],
        compiler_params=PARAMS,
    )(jnp.transpose(partners), *[pltpu.with_memory_space_constraint(v, pltpu.MemorySpace.HBM) for v in (x, positions)])
    z1, z2, z3 = [send(x, lambda c, s: (c, s ^ k)) for k in (1, 2, 3)]
    co, yo = [send(x, lambda c, s: (c ^ k, s)) for k in (1, 2)]
    xv, lines, columns, z2, z3, z1, yo, co = lax.optimization_barrier((xv, lines, columns, z2, z3, z1, yo, co))
    cz = send(jnp.concatenate([z1, z2, z3]), lambda c, s: (c ^ 1, s))
    cyo = send(yo, lambda c, s: (c ^ 1, s))
    space = scratch(rows, width) + [pltpu.VMEM((4 * rows, width), x.dtype)]
    sums = jax.ShapeDtypeStruct(sums_shape(rows), f32)
    pair = jax.ShapeDtypeStruct(sums_shape(rows, 2), f32)
    across = pl.pallas_call(
        functools.partial(across_kernel, scale=scale),
        out_shape=pair,
        in_specs=[VMEM] * 7,
        out_specs=VMEM,
        scratch_shapes=space,
        compiler_params=PARAMS,
    )(yo, z1, z2, z3, cz, lines, columns)
    there = send(across, lambda c, s: (c ^ 2, s))
    here, own = pl.pallas_call(
        functools.partial(here_kernel, scale=scale),
        out_shape=[pair, sums],
        in_specs=[VMEM] * 10,
        out_specs=[VMEM] * 2,
        scratch_shapes=space,
        compiler_params=PARAMS,
    )(xv, co, yo, cyo, z1, z2, z3, cz, lines, columns)
    stacks = pl.pallas_call(
        join_kernel,
        out_shape=jax.ShapeDtypeStruct((3, rows, 2 * LAGS), f32),
        in_specs=[VMEM] * 3,
        out_specs=VMEM,
        compiler_params=PARAMS,
    )(own, here, there)
    return jnp.transpose(stacks, (1, 0, 2))


def body(traces, positions, partners):
    x = traces[0]
    me = lax.axis_index("sect")
    chan = lax.axis_index("chan")
    if lax.axis_size("chan") == 4 and lax.axis_size("sect") == 4:
        return stacks_by_flips(x, positions, partners)[None]
    targets = jnp.stack([me, partners[me, 0], partners[me, 1]])
    return stacks_anywhere(x, traces, positions, targets, me, chan)[None]


def solution(mesh):
    in_specs = (P(("days", "sect"), "chan", None), P(), P())
    out_specs = P(("days", "sect"), "chan", None, None)
    return jax.shard_map(body, mesh=mesh, in_specs=in_specs, out_specs=out_specs, check_vma=False)
```

```python
import functools
import math

import jax
import jax.numpy as jnp
from jax import lax
from jax.experimental import pallas as pl
from jax.experimental.pallas import tpu as pltpu
from jax.sharding import PartitionSpec as P

LAGS = 64
HALF = LAGS // 2
LANES = 128
TILE = 256
VMEM = pl.BlockSpec(memory_space=pltpu.VMEM)
SMEM = pl.BlockSpec(memory_space=pltpu.SMEM)
HBM = pl.BlockSpec(memory_space=pltpu.MemorySpace.HBM)


def build_windows(x, t_ref):
    rows, width = x.shape
    lane = lax.broadcasted_iota(jnp.int32, (rows, width), 1)
    zero = jnp.zeros_like(x)
    for lag in range(LAGS):
        shift = HALF - lag
        start = (2 * (lag % HALF) + lag // HALF) * rows
        moved = x
        if shift != 0:
            inside = (lane < width - shift) if shift > 0 else (lane >= -shift)
            moved = jnp.where(inside, pltpu.roll(x, (-shift) % width, 1), zero)
        t_ref[pl.ds(start, rows), :] = moved


def products(xq, t_ref, c_ref):
    power = jnp.zeros((xq.shape[0], LANES), jnp.float32)
    for n in range(t_ref.shape[0] // TILE):
        cols = slice(n * TILE, (n + 1) * TILE)
        c = lax.dot_general(
            xq, t_ref[cols, :], (((1,), (1,)), ((), ())), preferred_element_type=jnp.float32
        )
        c_ref[:, cols] = c
        for h in range(TILE // LANES):
            part = c[:, h * LANES : (h + 1) * LANES]
            power = power + part * part
    return power + pltpu.roll(power, LANES // 2, 1)


def column_of(row):
    return jnp.transpose(jnp.broadcast_to(row, (8, row.shape[1])))[:, 0:1]


def weigh(power, columns, own, w_ref, scale):
    w = scale * lax.rsqrt(power * (1.0 / LAGS) + 1e-6)
    ahead = columns >= own
    w_ref[0] = jnp.where(ahead, w, 0.0)
    w_ref[1] = jnp.where(ahead, 0.0, w)


def side_sums(c_ref, w_ref, low, high, put):
    ncol = c_ref.shape[1] // LANES
    for n in range(ncol):
        part = c_ref[low:high, n * LANES : (n + 1) * LANES]
        for side in range(2):
            put(side * ncol + n, jnp.sum(part * w_ref[side, low:high], axis=0, keepdims=True))


def by_channel(sums, rows):
    ncol = sums.shape[0] // 2
    turned = jnp.transpose(sums)
    return jnp.concatenate(
        [
            turned[p * rows : (p + 1) * rows, s * ncol : (s + 1) * ncol]
            for s in range(2)
            for p in range(2)
        ],
        axis=1,
    )


def stack_kernel(
    sel_ref, x_ref, g_ref, pos_ref, own_ref, o_ref, t_ref, c_ref, w_ref, acc_ref, *, nblk, scale
):
    rows = x_ref.shape[0]
    build_windows(x_ref[...], t_ref)
    own = own_ref[...]
    for k in range(3):
        q = sel_ref[k]
        acc_ref[...] = jnp.zeros_like(acc_ref)

        @pl.loop(0, nblk)
        def _(b):
            power = products(g_ref[q, pl.ds(b * TILE, TILE), :], t_ref, c_ref)
            columns = column_of(pos_ref[q, :, pl.ds(b * TILE, TILE)])
            weigh(power, columns, own, w_ref, scale)

            def put(row, value):
                acc_ref[pl.ds(row, 1), :] += value

            side_sums(c_ref, w_ref, 0, TILE, put)

        o_ref[:, k, :] = by_channel(acc_ref[...], rows)


def scratch(rows, width, count):
    return [
        pltpu.VMEM((LAGS * rows, width), jnp.bfloat16),
        pltpu.VMEM((count, LAGS * rows), jnp.float32),
        pltpu.VMEM((2, count, LANES), jnp.float32),
    ]


def sums_shape(rows, count=None):
    shape = (2 * LAGS * rows // LANES, LANES)
    return shape if count is None else (count,) + shape


PARAMS = pltpu.CompilerParams(vmem_limit_bytes=48 << 20)


def stacks_anywhere(x, traces, positions, targets, me, chan):
    rows, width = x.shape
    chans, sections = lax.axis_size("chan"), lax.axis_size("sect")
    count = chans * rows
    whole = lax.all_gather(x, "chan", axis=0, tiled=True)
    whole = lax.all_gather(whole[None], "sect", axis=0, tiled=True)
    places = positions.astype(jnp.float32)
    own = lax.dynamic_slice(places, (me, chan * rows), (1, rows))
    own = jnp.concatenate([own, own], axis=1)
    return pl.pallas_call(
        functools.partial(stack_kernel, nblk=count // TILE, scale=1.0 / math.sqrt(count)),
        out_shape=jax.ShapeDtypeStruct((rows, 3, 2 * LAGS), jnp.float32),
        in_specs=[SMEM] + [VMEM] * 4,
        out_specs=VMEM,
        scratch_shapes=scratch(rows, width, TILE) + [pltpu.VMEM(sums_shape(rows), jnp.float32)],
        compiler_params=PARAMS,
    )(targets, x, whole, places.reshape(sections, 1, count), own)


def place_row(pos_ref, q):
    every = pos_ref[...].astype(jnp.float32)
    at = lax.broadcasted_iota(jnp.int32, every.shape, 0)
    return jnp.sum(jnp.where(at == q, every, 0.0), axis=0, keepdims=True)


def half_row(row, half):
    return jnp.where(half == 0, row[:, :LANES], row[:, LANES:])


def twice(row, core):
    turned = pltpu.roll(row, LANES // 2, 1)
    low = lax.broadcasted_iota(jnp.int32, row.shape, 1) // (LANES // 2)
    return jnp.where(low == core, row, turned)


def where_am_i():
    me, chan = lax.axis_index("sect"), lax.axis_index("chan")
    return me, chan // 2, chan % 2


def first_kernel(
    partners_ref, x_ref, pos_ref, xv_ref, rows_ref, cols_ref, o_ref, t_ref, c_ref, w_ref, places_ref, sems, *, scale
):
    me, half, core = where_am_i()
    rows = x_ref.shape[0]
    get_x = pltpu.make_async_copy(x_ref, xv_ref, sems.at[0])
    get_places = pltpu.make_async_copy(pos_ref, places_ref, sems.at[1])
    get_x.start()
    get_places.start()
    get_places.wait()
    row = place_row(places_ref, me)
    ours = twice(half_row(row, half), core)
    across = twice(half_row(row, 1 - half), core)
    rows_ref[0:1, :] = ours
    rows_ref[1:2, :] = across
    whose = [partners_ref[k, me] for k in range(2)]
    for k in range(2):
        rows_ref[2 + k : 3 + k, :] = jnp.full((1, LANES), whose[k] ^ me, jnp.int32).astype(jnp.float32)
        near = column_of(half_row(place_row(places_ref, whose[k]), half))
        cols_ref[2 * rows * k : 2 * rows * (k + 1), :] = jnp.broadcast_to(near, (2 * rows, LANES))
    others = (twice(half_row(row, half), 1 - core), across, twice(half_row(row, 1 - half), 1 - core))
    for k, other in enumerate(others):
        at = slice((4 + k) * rows, (5 + k) * rows)
        cols_ref[at, :] = jnp.broadcast_to(column_of(other)[:rows], (rows, LANES))
    get_x.wait()
    x = xv_ref[...]
    build_windows(x, t_ref)
    power = products(x, t_ref, c_ref)
    weigh(power, column_of(ours)[:rows], ours, w_ref, scale)

    def put(at, value):
        o_ref[at : at + 1, :] = value

    side_sums(c_ref, w_ref, 0, rows, put)


def gather_pairs(mine, peers, rows_ref, xs_ref, rows):
    core = lax.axis_index("chan") % 2
    for k in range(2):
        away = rows_ref[2 + k : 3 + k, :]
        picks = [(away == 1.0 + z).astype(jnp.bfloat16) for z in range(3)]
        for w in range(xs_ref.shape[1] // LANES):
            cut = slice(w * LANES, (w + 1) * LANES)
            own = sum(ref[:, cut] * pick for ref, pick in zip(mine, picks))
            peer = sum(peers[z * rows : (z + 1) * rows, cut] * pick for z, pick in enumerate(picks))
            low = pl.multiple_of((2 * k + core) * rows, rows)
            high = pl.multiple_of((2 * k + 1 - core) * rows, rows)
            xs_ref[pl.ds(low, rows), cut] = own
            xs_ref[pl.ds(high, rows), cut] = peer


def target_sums(xs_ref, t_ref, c_ref, w_ref, ours, cols_ref, o_ref, scale):
    count = xs_ref.shape[0]
    power = products(xs_ref[...], t_ref, c_ref)
    weigh(power, cols_ref[0:count, :], ours, w_ref, scale)
    edges = [e for e in (0, LANES, 2 * LANES, count) if e <= count]
    for k, (low, high) in enumerate(zip(edges[:-1], edges[1:])):
        if low == high:
            continue

        def put(at, value):
            o_ref[k, at : at + 1, :] = value

        side_sums(c_ref, w_ref, low, high, put)


def across_kernel(
    yo_ref, z1_ref, z2_ref, z3_ref, cz_ref, rows_ref, cols_ref, o_ref, t_ref, c_ref, w_ref, xs_ref, *, scale
):
    rows = yo_ref.shape[0]
    build_windows(yo_ref[...], t_ref)
    gather_pairs((z1_ref, z2_ref, z3_ref), cz_ref, rows_ref, xs_ref, rows)
    target_sums(xs_ref, t_ref, c_ref, w_ref, rows_ref[1:2, :], cols_ref, o_ref, scale)


def here_kernel(
    x_ref, co_ref, yo_ref, cyo_ref, z1_ref, z2_ref, z3_ref, cz_ref, rows_ref, cols_ref, o_ref, t_ref, c_ref, w_ref, xs_ref, *, scale
):
    rows = x_ref.shape[0]
    build_windows(x_ref[...], t_ref)
    gather_pairs((z1_ref, z2_ref, z3_ref), cz_ref, rows_ref, xs_ref, rows)
    for k, ref in enumerate((co_ref, yo_ref, cyo_ref)):
        xs_ref[(4 + k) * rows : (5 + k) * rows, :] = ref[...]
    target_sums(xs_ref, t_ref, c_ref, w_ref, rows_ref[0:1, :], cols_ref, o_ref, scale)


def join_kernel(own_ref, here_ref, there_ref, o_ref):
    rows = o_ref.shape[1]
    o_ref[0] = by_channel(own_ref[...] + here_ref[2], rows)
    for k in range(2):
        o_ref[1 + k] = by_channel(here_ref[k] + there_ref[k], rows)


def send(x, to):
    chans, sections = lax.axis_size("chan"), lax.axis_size("sect")
    pairs = []
    for c in range(chans):
        for s in range(sections):
            c2, s2 = to(c, s)
            pairs.append((c * sections + s, c2 * sections + s2))
    return lax.ppermute(x, ("chan", "sect"), pairs)


def stacks_by_flips(x, positions, partners):
    rows, width = x.shape
    scale = 1.0 / math.sqrt(4 * rows)
    sums = lambda *count: jax.ShapeDtypeStruct(sums_shape(rows, *count), jnp.float32)
    space = lambda blocks: scratch(rows, width, blocks * rows) + [pltpu.VMEM((blocks * rows, width), x.dtype)]
    xv, lines, columns, near = pl.pallas_call(
        functools.partial(first_kernel, scale=scale),
        out_shape=[
            jax.ShapeDtypeStruct(x.shape, x.dtype),
            jax.ShapeDtypeStruct((8, LANES), jnp.float32),
            jax.ShapeDtypeStruct((7 * rows, LANES), jnp.float32),
            sums(),
        ],
        in_specs=[SMEM, HBM, HBM],
        out_specs=[VMEM] * 4,
        scratch_shapes=scratch(rows, width, rows)
        + [pltpu.VMEM(positions.shape, positions.dtype), pltpu.SemaphoreType.DMA((2,))],
        compiler_params=PARAMS,
    )(jnp.transpose(partners), *[pltpu.with_memory_space_constraint(v, pltpu.MemorySpace.HBM) for v in (x, positions)])
    z1, z2, z3 = [send(x, lambda c, s: (c, s ^ k)) for k in (1, 2, 3)]
    co, yo = [send(x, lambda c, s: (c ^ k, s)) for k in (1, 2)]
    xv, lines, columns, near, z2, z3, z1, yo, co = lax.optimization_barrier((xv, lines, columns, near, z2, z3, z1, yo, co))
    cz = send(jnp.concatenate([z1, z2, z3]), lambda c, s: (c ^ 1, s))
    cyo = send(yo, lambda c, s: (c ^ 1, s))
    across = pl.pallas_call(
        functools.partial(across_kernel, scale=scale),
        out_shape=sums(2),
        in_specs=[VMEM] * 7,
        out_specs=VMEM,
        scratch_shapes=space(4),
        compiler_params=PARAMS,
    )(yo, z1, z2, z3, cz, lines, columns)
    there = send(across, lambda c, s: (c ^ 2, s))
    here = pl.pallas_call(
        functools.partial(here_kernel, scale=scale),
        out_shape=sums(3),
        in_specs=[VMEM] * 10,
        out_specs=VMEM,
        scratch_shapes=space(7),
        compiler_params=PARAMS,
    )(xv, co, yo, cyo, z1, z2, z3, cz, lines, columns)
    stacks = pl.pallas_call(
        join_kernel,
        out_shape=jax.ShapeDtypeStruct((3, rows, 2 * LAGS), jnp.float32),
        in_specs=[VMEM] * 3,
        out_specs=VMEM,
        compiler_params=PARAMS,
    )(near, here, there)
    return jnp.transpose(stacks, (1, 0, 2))


def body(traces, positions, partners):
    x = traces[0]
    me = lax.axis_index("sect")
    chan = lax.axis_index("chan")
    if lax.axis_size("chan") == 4 and lax.axis_size("sect") == 4:
        return stacks_by_flips(x, positions, partners)[None]
    targets = jnp.stack([me, partners[me, 0], partners[me, 1]])
    return stacks_anywhere(x, traces, positions, targets, me, chan)[None]


def solution(mesh):
    in_specs = (P(("days", "sect"), "chan", None), P(), P())
    out_specs = P(("days", "sect"), "chan", None, None)
    return jax.shard_map(body, mesh=mesh, in_specs=in_specs, out_specs=out_specs, check_vma=False)
```

```python
import functools
import math

import jax
import jax.numpy as jnp
from jax import lax
from jax.experimental import pallas as pl
from jax.experimental.pallas import tpu as pltpu
from jax.sharding import PartitionSpec as P

LAGS = 64
HALF = LAGS // 2
LANES = 128
TILE = 256
VMEM = pl.BlockSpec(memory_space=pltpu.VMEM)
SMEM = pl.BlockSpec(memory_space=pltpu.SMEM)
HBM = pl.BlockSpec(memory_space=pltpu.MemorySpace.HBM)


def build_windows(x, t_ref):
    rows, width = x.shape
    lane = lax.broadcasted_iota(jnp.int32, (rows, width), 1)
    zero = jnp.zeros_like(x)
    for lag in range(LAGS):
        shift = HALF - lag
        start = (2 * (lag % HALF) + lag // HALF) * rows
        moved = x
        if shift != 0:
            inside = (lane < width - shift) if shift > 0 else (lane >= -shift)
            moved = jnp.where(inside, pltpu.roll(x, (-shift) % width, 1), zero)
        t_ref[pl.ds(start, rows), :] = moved


def products(xq, t_ref, c_ref):
    power = jnp.zeros((xq.shape[0], LANES), jnp.float32)
    for n in range(t_ref.shape[0] // TILE):
        cols = slice(n * TILE, (n + 1) * TILE)
        c = lax.dot_general(
            xq, t_ref[cols, :], (((1,), (1,)), ((), ())), preferred_element_type=jnp.float32
        )
        c_ref[:, cols] = c
        for h in range(TILE // LANES):
            part = c[:, h * LANES : (h + 1) * LANES]
            power = power + part * part
    return power + pltpu.roll(power, LANES // 2, 1)


def column_of(row):
    return jnp.transpose(jnp.broadcast_to(row, (8, row.shape[1])))[:, 0:1]


def weigh(power, columns, own, w_ref, scale):
    w = scale * lax.rsqrt(power * (1.0 / LAGS) + 1e-6)
    ahead = columns >= own
    w_ref[0] = jnp.where(ahead, w, 0.0)
    w_ref[1] = jnp.where(ahead, 0.0, w)


def side_sums(c_ref, w_ref, low, high, put):
    ncol = c_ref.shape[1] // LANES
    for n in range(ncol):
        part = c_ref[low:high, n * LANES : (n + 1) * LANES]
        for side in range(2):
            put(side * ncol + n, jnp.sum(part * w_ref[side, low:high], axis=0, keepdims=True))


def by_channel(sums, rows):
    ncol = sums.shape[0] // 2
    turned = jnp.transpose(sums)
    return jnp.concatenate(
        [
            turned[p * rows : (p + 1) * rows, s * ncol : (s + 1) * ncol]
            for s in range(2)
            for p in range(2)
        ],
        axis=1,
    )


def stack_kernel(
    sel_ref, x_ref, g_ref, pos_ref, own_ref, o_ref, t_ref, c_ref, w_ref, acc_ref, *, nblk, scale
):
    rows = x_ref.shape[0]
    build_windows(x_ref[...], t_ref)
    own = own_ref[...]
    for k in range(3):
        q = sel_ref[k]
        acc_ref[...] = jnp.zeros_like(acc_ref)

        @pl.loop(0, nblk)
        def _(b):
            power = products(g_ref[q, pl.ds(b * TILE, TILE), :], t_ref, c_ref)
            columns = column_of(pos_ref[q, :, pl.ds(b * TILE, TILE)])
            weigh(power, columns, own, w_ref, scale)

            def put(row, value):
                acc_ref[pl.ds(row, 1), :] += value

            side_sums(c_ref, w_ref, 0, TILE, put)

        o_ref[:, k, :] = by_channel(acc_ref[...], rows)


def scratch(rows, width, count):
    return [
        pltpu.VMEM((LAGS * rows, width), jnp.bfloat16),
        pltpu.VMEM((count, LAGS * rows), jnp.float32),
        pltpu.VMEM((2, count, LANES), jnp.float32),
    ]


def sums_shape(rows, count=None):
    shape = (2 * LAGS * rows // LANES, LANES)
    return shape if count is None else (count,) + shape


PARAMS = pltpu.CompilerParams(vmem_limit_bytes=48 << 20)


def stacks_anywhere(x, traces, positions, targets, me, chan):
    rows, width = x.shape
    chans, sections = lax.axis_size("chan"), lax.axis_size("sect")
    count = chans * rows
    whole = lax.all_gather(x, "chan", axis=0, tiled=True)
    whole = lax.all_gather(whole[None], "sect", axis=0, tiled=True)
    places = positions.astype(jnp.float32)
    own = lax.dynamic_slice(places, (me, chan * rows), (1, rows))
    own = jnp.concatenate([own, own], axis=1)
    return pl.pallas_call(
        functools.partial(stack_kernel, nblk=count // TILE, scale=1.0 / math.sqrt(count)),
        out_shape=jax.ShapeDtypeStruct((rows, 3, 2 * LAGS), jnp.float32),
        in_specs=[SMEM] + [VMEM] * 4,
        out_specs=VMEM,
        scratch_shapes=scratch(rows, width, TILE) + [pltpu.VMEM(sums_shape(rows), jnp.float32)],
        compiler_params=PARAMS,
    )(targets, x, whole, places.reshape(sections, 1, count), own)


def place_row(pos_ref, q):
    every = pos_ref[...].astype(jnp.float32)
    at = lax.broadcasted_iota(jnp.int32, every.shape, 0)
    return jnp.sum(jnp.where(at == q, every, 0.0), axis=0, keepdims=True)


def half_row(row, half):
    return jnp.where(half == 0, row[:, :LANES], row[:, LANES:])


def twice(row, core):
    turned = pltpu.roll(row, LANES // 2, 1)
    low = lax.broadcasted_iota(jnp.int32, row.shape, 1) // (LANES // 2)
    return jnp.where(low == core, row, turned)


def where_am_i():
    me, chan = lax.axis_index("sect"), lax.axis_index("chan")
    return me, chan // 2, chan % 2


def first_kernel(
    partners_ref, x_ref, pos_ref, xv_ref, rows_ref, cols_ref, o_ref, t_ref, c_ref, w_ref, places_ref, sems, *, scale
):
    me, half, core = where_am_i()
    rows = x_ref.shape[0]
    get_x = pltpu.make_async_copy(x_ref, xv_ref, sems.at[0])
    get_places = pltpu.make_async_copy(pos_ref, places_ref, sems.at[1])
    get_x.start()
    get_places.start()
    get_places.wait()
    row = place_row(places_ref, me)
    ours = twice(half_row(row, half), core)
    across = twice(half_row(row, 1 - half), core)
    rows_ref[0:1, :] = ours
    rows_ref[1:2, :] = across
    whose = [partners_ref[k, me] for k in range(2)]
    for k in range(2):
        rows_ref[2 + k : 3 + k, :] = jnp.full((1, LANES), whose[k] ^ me, jnp.int32).astype(jnp.float32)
        near = column_of(half_row(place_row(places_ref, whose[k]), half))
        cols_ref[2 * rows * k : 2 * rows * (k + 1), :] = jnp.broadcast_to(near, (2 * rows, LANES))
    others = (twice(half_row(row, half), 1 - core), across, twice(half_row(row, 1 - half), 1 - core))
    for k, other in enumerate(others):
        at = slice((4 + k) * rows, (5 + k) * rows)
        cols_ref[at, :] = jnp.broadcast_to(column_of(other)[:rows], (rows, LANES))
    get_x.wait()
    x = xv_ref[...]
    build_windows(x, t_ref)
    power = products(x, t_ref, c_ref)
    weigh(power, column_of(ours)[:rows], ours, w_ref, scale)

    def put(at, value):
        o_ref[at : at + 1, :] = value

    side_sums(c_ref, w_ref, 0, rows, put)


def gather_pairs(mine, peers, rows_ref, xs_ref, rows):
    core = lax.axis_index("chan") % 2
    for k in range(2):
        away = rows_ref[2 + k : 3 + k, :]
        picks = [(away == 1.0 + z).astype(jnp.bfloat16) for z in range(3)]
        for w in range(xs_ref.shape[1] // LANES):
            cut = slice(w * LANES, (w + 1) * LANES)
            own = sum(ref[:, cut] * pick for ref, pick in zip(mine, picks))
            peer = sum(peers[z * rows : (z + 1) * rows, cut] * pick for z, pick in enumerate(picks))
            low = pl.multiple_of((2 * k + core) * rows, rows)
            high = pl.multiple_of((2 * k + 1 - core) * rows, rows)
            xs_ref[pl.ds(low, rows), cut] = own
            xs_ref[pl.ds(high, rows), cut] = peer


def target_sums(xs_ref, t_ref, c_ref, w_ref, ours, cols_ref, o_ref, scale):
    count = xs_ref.shape[0]
    power = products(xs_ref[...], t_ref, c_ref)
    weigh(power, cols_ref[0:count, :], ours, w_ref, scale)
    edges = [e for e in (0, LANES, 2 * LANES, count) if e <= count]
    for k, (low, high) in enumerate(zip(edges[:-1], edges[1:])):
        if low == high:
            continue

        def put(at, value):
            o_ref[k, at : at + 1, :] = value

        side_sums(c_ref, w_ref, low, high, put)


def across_kernel(
    yo_ref, z1_ref, z2_ref, z3_ref, cz_ref, rows_ref, cols_ref, o_ref, xs_ref, t_ref, c_ref, w_ref, *, scale
):
    rows = yo_ref.shape[0]
    build_windows(yo_ref[...], t_ref)
    gather_pairs((z1_ref, z2_ref, z3_ref), cz_ref, rows_ref, xs_ref, rows)
    target_sums(xs_ref, t_ref, c_ref, w_ref, rows_ref[1:2, :], cols_ref, o_ref, scale)


def here_kernel(
    x_ref, co_ref, yo_ref, cyo_ref, picked_ref, rows_ref, cols_ref, o_ref, t_ref, c_ref, w_ref, xs_ref, *, scale
):
    rows = x_ref.shape[0]
    build_windows(x_ref[...], t_ref)
    xs_ref[0 : 4 * rows, :] = picked_ref[...]
    for k, ref in enumerate((co_ref, yo_ref, cyo_ref)):
        xs_ref[(4 + k) * rows : (5 + k) * rows, :] = ref[...]
    target_sums(xs_ref, t_ref, c_ref, w_ref, rows_ref[0:1, :], cols_ref, o_ref, scale)


def join_kernel(own_ref, here_ref, there_ref, o_ref):
    rows = o_ref.shape[1]
    o_ref[0] = by_channel(own_ref[...] + here_ref[2], rows)
    for k in range(2):
        o_ref[1 + k] = by_channel(here_ref[k] + there_ref[k], rows)


def send(x, to):
    chans, sections = lax.axis_size("chan"), lax.axis_size("sect")
    pairs = []
    for c in range(chans):
        for s in range(sections):
            c2, s2 = to(c, s)
            pairs.append((c * sections + s, c2 * sections + s2))
    return lax.ppermute(x, ("chan", "sect"), pairs)


def stacks_by_flips(x, positions, partners):
    rows, width = x.shape
    scale = 1.0 / math.sqrt(4 * rows)
    sums = lambda *count: jax.ShapeDtypeStruct(sums_shape(rows, *count), jnp.float32)
    space = lambda blocks: scratch(rows, width, blocks * rows) + [pltpu.VMEM((blocks * rows, width), x.dtype)]
    xv, lines, columns, near = pl.pallas_call(
        functools.partial(first_kernel, scale=scale),
        out_shape=[
            jax.ShapeDtypeStruct(x.shape, x.dtype),
            jax.ShapeDtypeStruct((8, LANES), jnp.float32),
            jax.ShapeDtypeStruct((7 * rows, LANES), jnp.float32),
            sums(),
        ],
        in_specs=[SMEM, HBM, HBM],
        out_specs=[VMEM] * 4,
        scratch_shapes=scratch(rows, width, rows)
        + [pltpu.VMEM(positions.shape, positions.dtype), pltpu.SemaphoreType.DMA((2,))],
        compiler_params=PARAMS,
    )(jnp.transpose(partners), *[pltpu.with_memory_space_constraint(v, pltpu.MemorySpace.HBM) for v in (x, positions)])
    z1, z2, z3 = [send(x, lambda c, s: (c, s ^ k)) for k in (1, 2, 3)]
    co, yo = [send(x, lambda c, s: (c ^ k, s)) for k in (1, 2)]
    xv, lines, columns, near, z2, z3, z1, yo, co = lax.optimization_barrier((xv, lines, columns, near, z2, z3, z1, yo, co))
    cz = send(jnp.concatenate([z1, z2, z3]), lambda c, s: (c ^ 1, s))
    cyo = send(yo, lambda c, s: (c ^ 1, s))
    across, picked = pl.pallas_call(
        functools.partial(across_kernel, scale=scale),
        out_shape=[sums(2), jax.ShapeDtypeStruct((4 * rows, width), x.dtype)],
        in_specs=[VMEM] * 7,
        out_specs=[VMEM] * 2,
        scratch_shapes=scratch(rows, width, 4 * rows),
        compiler_params=PARAMS,
    )(yo, z1, z2, z3, cz, lines, columns)
    there = send(across, lambda c, s: (c ^ 2, s))
    here = pl.pallas_call(
        functools.partial(here_kernel, scale=scale),
        out_shape=sums(3),
        in_specs=[VMEM] * 7,
        out_specs=VMEM,
        scratch_shapes=space(7),
        compiler_params=PARAMS,
    )(xv, co, yo, cyo, picked, lines, columns)
    stacks = pl.pallas_call(
        join_kernel,
        out_shape=jax.ShapeDtypeStruct((3, rows, 2 * LAGS), jnp.float32),
        in_specs=[VMEM] * 3,
        out_specs=VMEM,
        compiler_params=PARAMS,
    )(near, here, there)
    return jnp.transpose(stacks, (1, 0, 2))


def body(traces, positions, partners):
    x = traces[0]
    me = lax.axis_index("sect")
    chan = lax.axis_index("chan")
    if lax.axis_size("chan") == 4 and lax.axis_size("sect") == 4:
        return stacks_by_flips(x, positions, partners)[None]
    targets = jnp.stack([me, partners[me, 0], partners[me, 1]])
    return stacks_anywhere(x, traces, positions, targets, me, chan)[None]


def solution(mesh):
    in_specs = (P(("days", "sect"), "chan", None), P(), P())
    out_specs = P(("days", "sect"), "chan", None, None)
    return jax.shard_map(body, mesh=mesh, in_specs=in_specs, out_specs=out_specs, check_vma=False)
```
